256 devices in a mesh: dp: 2 (over core), seq: 16 (over y, x), head: 8 (over z).
Axes of the slice: x: 4, y: 4, z: 8, core: 2. Of those that a mesh axis runs over, the one named last changes fastest.
Arguments:
- query_rows: bfloat16 [2, 8192, 8192], P('dp', 'seq', 'head'), may hold values from -1.796875 to 1.796875
- key_rows: bfloat16 [2, 8192, 8192], P('dp', 'seq', 'head'), may hold values from -1.796875 to 1.796875
- value_rows: bfloat16 [2, 8192, 8192], P('dp', 'seq', 'head'), may hold values from -6 to 6
- norm_gain: float32 [8192], P('head'), may hold values from 0.1 to 1.9
- cotangent: bfloat16 [2, 8192, 8192], P('dp', 'seq', 'head'), may hold values from -10 to 10
- loss_mask: int32 [2, 8192], P('dp', 'seq'), may hold values 0 or 1
- importance: float32 [2, 8192], P('dp', 'seq'), may hold values from 0.5 to 2
- advantage: float32 [2], P('dp'), may hold values from -3 to 3
- lengths: int32 [2], P('dp'), may hold values from 2048 to 8192, as said below
- decay_index: int32 [64], P('head'), may hold values from 0 to 11
Outputs:
- mixed: bfloat16 [2, 8192, 8192], P('dp', 'seq', 'head')
- query_grad: bfloat16 [2, 8192, 8192], P('dp', 'seq', 'head')
- key_grad: bfloat16 [2, 8192, 8192], P('dp', 'seq', 'head')
- value_grad: bfloat16 [2, 8192, 8192], P('dp', 'seq', 'head')
- gain_grad: float32 [8192], P('head')
The draws below stay inside these ranges and needn't reach their ends.
Inputs may be any that keep to these rules, and one draw needn't show every extreme that they name: `lengths`: at least one response has length 8192.
All inputs are finite; a program needn't handle non-finite values. No bound on the sum of `loss_mask` on one device may be relied on, other than what follows from the above.
Results may differ from the reference program's by a relative error of at most 0.0063.
Values sent between devices are 32-bit elements; how exact they have to be, the bound alone decides.
No kernel may reach another device: no remote copies, remote signals or barrier semaphores. Data moves between devices by JAX's collectives and lax.ppermute only.
A program may use at most 128 MiB of HBM per device.

```python
import math
import jax
import jax.numpy as jnp
from jax import lax

HEAD_DIM = 128
TOK_DEV = 512
HEADS = 64
SEQ_LEN = 8192
BATCH = 2
N_SEQ = 16


def draw_cotangent(key, part):
    features = HEADS * HEAD_DIM
    order = jnp.arange(BATCH * SEQ_LEN, dtype=jnp.float32).reshape(BATCH, SEQ_LEN, 1)
    scale = 0.5 + order / (BATCH * SEQ_LEN - 1)
    base = jnp.clip(jax.random.normal(jax.random.fold_in(key, 13), (BATCH, SEQ_LEN, features), jnp.float32), -6.0, 6.0)
    values = base * scale
    return values.astype(jnp.bfloat16)


def draw_lengths(key, part):
    base = jax.random.randint(jax.random.fold_in(key, 21), (BATCH,), SEQ_LEN // 4, SEQ_LEN + 1, dtype=jnp.int32)
    chosen = jax.random.randint(jax.random.fold_in(key, 22), (), 0, BATCH, dtype=jnp.int32)
    rows = jnp.arange(BATCH, dtype=jnp.int32)
    return jnp.where(rows == chosen, jnp.int32(SEQ_LEN), base).astype(jnp.int32)


def place_ends(result, rng, smallest, largest):
    index_at = [jax.random.randint(jax.random.fold_in(rng, axis), (), 0, length) for axis, length in enumerate(result.shape)]
    main_axis = result.shape.index(max(result.shape))
    neighbour = index_at[:main_axis] + [(index_at[main_axis] + 1) % result.shape[main_axis]] + index_at[main_axis + 1:]
    return result.at[tuple(index_at)].set(smallest).at[tuple(neighbour)].set(largest)


def shard_levels(key, shape, split, least, top_value):
    def one(axis_at, blocks):
        steps = jax.random.uniform(jax.random.fold_in(jax.random.fold_in(key, 6), axis_at), (blocks,), jnp.float32, least / len(split), top_value / len(split))
        return jnp.repeat(jnp.exp(steps), shape[axis_at] // blocks).reshape((-1,) + (1,) * (len(shape) - axis_at - 1))

    factor_of = one(*split[0])
    for cut in split[1:]:
        factor_of = factor_of * one(*cut)
    return factor_of


def centred(stream_key, dims, scale, most, shards=(), held_as=jnp.bfloat16):
    loudness = shard_levels(stream_key, dims, shards, -0.22, 0.18) if shards else 1.0
    result = jax.random.normal(stream_key, dims, jnp.float32) * scale * loudness
    return jnp.minimum(jnp.maximum(result, -most), most).astype(held_as)


def setup_inputs(seed: int = 0) -> dict:
    streams_of = jax.random.split(jax.random.key(seed), 11)
    return {
        "query_rows": centred(streams_of[0], (BATCH, SEQ_LEN, HEADS * HEAD_DIM), 0.3, 1.796875, ((0, 2), (1, 16), (2, 8))),
        "key_rows": centred(streams_of[1], (BATCH, SEQ_LEN, HEADS * HEAD_DIM), 0.3, 1.796875, ((0, 2), (1, 16), (2, 8))),
        "value_rows": centred(streams_of[2], (BATCH, SEQ_LEN, HEADS * HEAD_DIM), 1.0, 6.0, ((0, 2), (1, 16), (2, 8))),
        "norm_gain": jnp.clip(1.0 + 0.18 * jax.random.normal(streams_of[3], (HEADS * HEAD_DIM,), jnp.float32), 0.1, 1.9),
        "cotangent": draw_cotangent(jax.random.fold_in(streams_of[10], 71), 0),
        "loss_mask": place_ends((jax.random.randint(streams_of[5], (BATCH, SEQ_LEN), 0, 4) < 3).astype(jnp.int32), jax.random.fold_in(streams_of[5], 1), 0, 1),
        "importance": jnp.clip(jnp.exp(math.log(2.0) - 1.3862944 * jax.random.uniform(streams_of[6], (BATCH, SEQ_LEN), jnp.float32) ** shard_levels(streams_of[6], (BATCH, SEQ_LEN), ((0, 2), (1, 16)), -0.2, 0.2)), 0.5, 2.0),
        "advantage": centred(streams_of[7], (BATCH,), 1.0, 3.0, ((0, 2),), jnp.float32),
        "lengths": draw_lengths(jax.random.fold_in(streams_of[10], 71), 0),
        "decay_index": place_ends(jax.random.randint(streams_of[9], (HEADS,), 0, 12), jax.random.fold_in(streams_of[9], 1), 0, 11).astype(jnp.int32),
    }


clip_high = 1.28
epsilon = 1e-06

def head_rates(decay_index):
    return 16.0 / (TOK_DEV * jnp.exp2(decay_index.astype(jnp.float32)))

def by_heads(array):
    return array.reshape(BATCH, N_SEQ, TOK_DEV, HEADS, HEAD_DIM).transpose(3, 0, 1, 2, 4)

def merge_heads(array):
    return array.transpose(1, 2, 3, 0, 4).reshape(BATCH, SEQ_LEN, HEADS * HEAD_DIM)

def decay_table(decay_rate):
    offsets = jnp.arange(TOK_DEV, dtype=jnp.float32)
    lagged = offsets[:, None] - offsets[None, :]
    within = jnp.where(lagged >= 0, jnp.exp2(-decay_rate * jnp.maximum(lagged, 0.0)), 0.0)
    return (offsets, within)

def carry_states(local_terms, factor, reverse):

    def advance(running, local_term):
        return (factor * running + local_term, running)
    zeros_state = jnp.zeros(local_terms.shape[1:], jnp.float32)
    _, passed = lax.scan(advance, zeros_state, local_terms, reverse=reverse)
    return passed

def forward_parts(queries, key_heads, value_heads, decay_rate):
    offsets, within = decay_table(decay_rate)
    scores = jnp.einsum('bntd,bnsd->bnts', queries.astype(jnp.float32), key_heads.astype(jnp.float32))
    score_half = (scores * within).astype(jnp.bfloat16)
    key_decayed = (key_heads.astype(jnp.float32) * jnp.exp2(-decay_rate * (TOK_DEV - 1 - offsets))[:, None]).astype(jnp.bfloat16)
    state_local = jnp.einsum('bntd,bnte->bnde', key_decayed.astype(jnp.float32), value_heads.astype(jnp.float32))
    passed = carry_states(state_local.transpose(1, 0, 2, 3), jnp.exp2(-decay_rate * TOK_DEV), False)
    state_half = passed.transpose(1, 0, 2, 3).astype(jnp.bfloat16)
    return (offsets, within, score_half, state_half)

def forward_head(queries, key_heads, value_heads, decay_rate):
    offsets, within, score_half, state_half = forward_parts(queries, key_heads, value_heads, decay_rate)
    local_out = jnp.einsum('bnts,bnse->bnte', score_half.astype(jnp.float32), value_heads.astype(jnp.float32))
    carried = jnp.einsum('bntd,bnde->bnte', queries.astype(jnp.float32), state_half.astype(jnp.float32))
    return local_out + carried * jnp.exp2(-decay_rate * (offsets + 1.0))[:, None]

def backward_head(queries, key_heads, value_heads, grad_heads, decay_rate):
    offsets, within, score_half, state_half = forward_parts(queries, key_heads, value_heads, decay_rate)
    f_query = queries.astype(jnp.float32)
    f_key = key_heads.astype(jnp.float32)
    f_value = value_heads.astype(jnp.float32)
    f_grad = grad_heads.astype(jnp.float32)
    dscore = (jnp.einsum('bnte,bnse->bnts', f_grad, f_value) * within).astype(jnp.bfloat16).astype(jnp.float32)
    query_decayed = (f_query * jnp.exp2(-decay_rate * offsets)[:, None]).astype(jnp.bfloat16)
    return_local = jnp.einsum('bntd,bnte->bnde', query_decayed.astype(jnp.float32), f_grad)
    passed = carry_states(return_local.transpose(1, 0, 2, 3), jnp.exp2(-decay_rate * TOK_DEV), True)
    return_half = passed.transpose(1, 0, 2, 3).astype(jnp.bfloat16).astype(jnp.float32)
    from_start = jnp.exp2(-decay_rate * (offsets + 1.0))[:, None]
    to_next = jnp.exp2(-decay_rate * (TOK_DEV - offsets))[:, None]
    query_grad = jnp.einsum('bnts,bnsd->bntd', dscore, f_key)
    query_grad = query_grad + jnp.einsum('bnte,bnde->bntd', f_grad, state_half.astype(jnp.float32)) * from_start
    key_grad = jnp.einsum('bnts,bntd->bnsd', dscore, f_query)
    key_grad = key_grad + jnp.einsum('bnte,bnde->bntd', f_value, return_half) * to_next
    value_grad = jnp.einsum('bnts,bnte->bnse', score_half.astype(jnp.float32), f_grad)
    value_grad = value_grad + jnp.einsum('bntd,bnde->bnte', f_key, return_half) * to_next
    return (query_grad, key_grad, value_grad)

def reference(query_rows, key_rows, value_rows, norm_gain, cotangent, loss_mask, importance, advantage, lengths, decay_index):
    decay_rates = head_rates(decay_index)
    query_heads = by_heads(query_rows)
    key_heads = by_heads(key_rows)
    value_heads = by_heads(value_rows)

    def forward_bundle(bundle):
        return forward_head(bundle[0], bundle[1], bundle[2], bundle[3])
    head_outs = lax.map(forward_bundle, (query_heads, key_heads, value_heads, decay_rates))
    outputs_flat = merge_heads(head_outs)
    features = HEADS * HEAD_DIM
    positions = jnp.arange(SEQ_LEN, dtype=jnp.int32)
    in_length = (positions[None, :] < lengths[:, None]).astype(jnp.float32)
    token_weight = loss_mask.astype(jnp.float32) * in_length * jnp.minimum(importance, clip_high)
    token_weight = token_weight * advantage[:, None] * (float(SEQ_LEN) / lengths.astype(jnp.float32))[:, None]
    grad_y = cotangent.astype(jnp.float32) * token_weight[..., None]
    grad_n = grad_y * norm_gain
    inverse = lax.rsqrt(lax.optimization_barrier(jnp.sum(outputs_flat * outputs_flat, -1)) / features + epsilon)
    normed = outputs_flat * inverse[..., None]
    mixed = (normed * norm_gain).astype(jnp.bfloat16)
    mean_term = lax.optimization_barrier(jnp.sum(grad_n * outputs_flat, -1)) * inverse / features
    grad_out = (inverse[..., None] * (grad_n - normed * mean_term[..., None])).astype(jnp.bfloat16)
    gain_grad = lax.optimization_barrier(jnp.sum(grad_y * normed, axis=(0, 1)))
    grad_heads = by_heads(grad_out)

    def backward_bundle(bundle):
        return backward_head(bundle[0], bundle[1], bundle[2], bundle[3], bundle[4])
    gradients = lax.map(backward_bundle, (query_heads, key_heads, value_heads, grad_heads, decay_rates))
    query_grad = merge_heads(gradients[0]).astype(jnp.bfloat16)
    key_grad = merge_heads(gradients[1]).astype(jnp.bfloat16)
    value_grad = merge_heads(gradients[2]).astype(jnp.bfloat16)
    return (mixed, query_grad, key_grad, value_grad, gain_grad)
```

```python
import functools

import jax
import jax.numpy as jnp
from jax import lax
from jax.experimental import pallas as pl
from jax.experimental.pallas import tpu as pltpu
from jax.sharding import PartitionSpec as P

clip_high = 1.28
epsilon = 1e-06
F32 = jnp.float32
BF16 = jnp.bfloat16
LANES = 128
HALF = 256


def dot_nn(a, b):
    return lax.dot_general(a, b, (((1,), (0,)), ((), ())), preferred_element_type=F32)


def dot_nt(a, b):
    return lax.dot_general(a, b, (((1,), (1,)), ((), ())), preferred_element_type=F32)


def dot_tn(a, b):
    return lax.dot_general(a, b, (((0,), (0,)), ((), ())), preferred_element_type=F32)


def rate_of(index, slab):
    return (16.0 / slab) * jnp.exp2(jnp.full((1, LANES), -index.astype(F32), F32))


def row_powers(rate, first, step, rows):
    at = lax.broadcasted_iota(jnp.int32, (rows, LANES), 0).astype(F32)
    return jnp.exp2(-rate * (first + step * at))


def decay_blocks(rate, transposed):
    rate2 = jnp.concatenate([rate] * (HALF // LANES), axis=1)
    rows = lax.broadcasted_iota(jnp.int32, (HALF, HALF), 0)
    cols = lax.broadcasted_iota(jnp.int32, (HALF, HALF), 1)
    lag = (cols - rows if transposed else rows - cols).astype(F32)
    diagonal = jnp.where(lag >= 0, jnp.exp2(-rate2 * jnp.maximum(lag, 0.0)), 0.0)
    below = jnp.exp2(-rate2 * (lag + float(HALF)))
    return diagonal, below


def to_columns(row):
    parts = []
    for at in range(0, row.shape[1], LANES):
        parts.append(jnp.broadcast_to(row[:, at : at + LANES], (LANES, LANES)).T)
    return jnp.concatenate(parts, axis=0)


def head(ref, i):
    return ref[0, :, i * LANES : (i + 1) * LANES]


def state_kernel(per_step, slab, index_ref, k_ref, v_ref, out_ref):
    for i in range(per_step):
        rate = rate_of(index_ref[pl.program_id(0) * per_step + i], slab)
        decayed = head(k_ref, i).astype(F32) * row_powers(rate, slab - 1.0, -1.0, slab)
        out_ref[i] = dot_tn(decayed.astype(BF16), head(v_ref, i))


def scan_kernel(slabs, slab, reverse, index_ref, x_ref, out_ref):
    rate = rate_of(index_ref[0], slab)
    factor = jnp.exp2(-rate * float(slab))
    running = jnp.zeros(x_ref.shape[1:], F32)
    for j in reversed(range(slabs)) if reverse else range(slabs):
        out_ref[j] = running
        running = factor * running + x_ref[j]


def scan_gain_kernel(slabs, slab, index_ref, x_ref, g_ref, out_ref):
    rate = rate_of(index_ref[0], slab)
    factor = jnp.exp2(-rate * float(slab))
    rows = x_ref.shape[1]
    running = jnp.zeros(x_ref.shape[1:], F32)
    for j in reversed(range(slabs)):
        out_ref[j, :rows] = running
        out_ref[j, rows:] = g_ref[...]
        running = factor * running + x_ref[j]


def local_kernel(
    per_step, slab, total, index_ref, place_ref, length_ref, advantage_ref, q_ref, k_ref, v_ref, mask_ref, imp_ref,
    out_ref, weight_ref,
):
    @pl.when(pl.program_id(0) == 0)
    def _():
        at = place_ref[0] * slab + lax.broadcasted_iota(jnp.int32, (1, slab), 1)
        inside = (at < length_ref[0]).astype(F32)
        length = jnp.full((1, slab), length_ref[0].astype(F32), F32)
        weight = mask_ref[...].astype(F32) * inside * jnp.minimum(imp_ref[...], clip_high)
        weight = weight * advantage_ref[0] * (float(total) / length)
        weight_ref[...] = to_columns(weight)

    for i in range(per_step):
        rate = rate_of(index_ref[pl.program_id(0) * per_step + i], slab)
        diagonal, below = decay_blocks(rate, False)
        q, k, v = head(q_ref, i), head(k_ref, i), head(v_ref, i)
        lanes = slice(i * LANES, (i + 1) * LANES)
        for r in range(slab // HALF):
            scores = dot_nt(q[r * HALF : (r + 1) * HALF], k[: (r + 1) * HALF])
            table = diagonal if r == 0 else jnp.concatenate([below, diagonal], axis=1)
            probs = (scores * table).astype(BF16)
            out_ref[r * HALF : (r + 1) * HALF, lanes] = dot_nn(probs, v[: (r + 1) * HALF])


def output_kernel(
    per_step, slab, index_ref, q_ref, s_ref, local_ref, c_ref, weight_ref, gain_ref, out_ref, stat_ref, square, cross
):
    step = pl.program_id(0)
    squares = jnp.zeros((slab, LANES), F32)
    crosses = jnp.zeros((slab, LANES), F32)
    for i in range(per_step):
        rate = rate_of(index_ref[step * per_step + i], slab)
        lanes = slice(i * LANES, (i + 1) * LANES)
        carried = dot_nn(head(q_ref, i), s_ref[i].astype(BF16))
        out = local_ref[:, lanes] + carried * row_powers(rate, 1.0, 1.0, slab)
        out_ref[:, lanes] = out
        grad_n = head(c_ref, i).astype(F32) * weight_ref[...] * gain_ref[:, lanes]
        squares += out * out
        crosses += grad_n * out

    @pl.when(step == 0)
    def _():
        square[...] = squares
        cross[...] = crosses

    @pl.when(step != 0)
    def _():
        square[...] += squares
        cross[...] += crosses

    @pl.when(step == pl.num_programs(0) - 1)
    def _():
        rows = []
        for ref in (square, cross):
            for at in range(0, slab, LANES):
                rows.append(jnp.sum(ref[at : at + LANES, :].T, axis=0, keepdims=True))
        stats = jnp.concatenate(rows, axis=0)
        for d in range(stat_ref.shape[0]):
            stat_ref[d] = stats


def grad_kernel(
    per_step, slab, features, index_ref, stat_ref, q_ref, o_ref, c_ref, weight_ref, gain_ref,
    g_ref, ret_ref, gain_out_ref, inv_ref, mean_ref, inv_col, mean_col,
):
    step = pl.program_id(0)

    @pl.when(step == 0)
    def _():
        stats = jnp.sum(stat_ref[...], axis=0)
        blocks = slab // LANES
        inverse = lax.rsqrt(stats[:blocks] / features + epsilon)
        mean = stats[blocks : 2 * blocks] * inverse / features
        for b in range(blocks):
            rows = slice(b * LANES, (b + 1) * LANES)
            inv_col[rows, :] = jnp.broadcast_to(inverse[b : b + 1], (LANES, LANES)).T
            mean_col[rows, :] = jnp.broadcast_to(mean[b : b + 1], (LANES, LANES)).T
        inv_ref[...] = inv_col[...]
        mean_ref[...] = mean_col[...]

    for i in range(per_step):
        rate = rate_of(index_ref[step * per_step + i], slab)
        lanes = slice(i * LANES, (i + 1) * LANES)
        inverse = inv_col[...]
        normed = o_ref[:, lanes] * inverse
        grad_y = head(c_ref, i).astype(F32) * weight_ref[...]
        grad_n = grad_y * gain_ref[:, lanes]
        grad_out = (inverse * (grad_n - normed * mean_col[...])).astype(BF16)
        g_ref[:, lanes] = grad_out
        gain_out_ref[pl.ds(step * per_step + i, 1), :] = jnp.sum(grad_y * normed, axis=0, keepdims=True)
        decayed = head(q_ref, i).astype(F32) * row_powers(rate, 0.0, 1.0, slab)
        ret_ref[i] = dot_tn(decayed.astype(BF16), grad_out)


def backward_kernel(
    per_step, slab, index_ref, q_ref, k_ref, v_ref, g_ref, s_ref, o_ref, inv_ref, gain_ref,
    mixed_ref, qg_ref, kl_ref, vl_ref,
):
    for i in range(per_step):
        rate = rate_of(index_ref[pl.program_id(0) * per_step + i], slab)
        lanes = slice(i * LANES, (i + 1) * LANES)
        mixed_ref[0, :, lanes] = (o_ref[:, lanes] * inv_ref[...] * gain_ref[:, lanes]).astype(BF16)
        q, k, v, g = head(q_ref, i), head(k_ref, i), head(v_ref, i), g_ref[:, lanes]
        diagonal, below = decay_blocks(rate, False)
        diagonal_t, below_t = decay_blocks(rate, True)
        carried = dot_nt(g, s_ref[i].astype(BF16)) * row_powers(rate, 1.0, 1.0, slab)
        a, b = slice(0, HALF), slice(HALF, 2 * HALF)
        upper = (dot_nt(g[a], v[a]) * diagonal).astype(BF16)
        lower = (dot_nt(g[b], v) * jnp.concatenate([below, diagonal], axis=1)).astype(BF16)
        qg_ref[0, a, lanes] = (dot_nn(upper, k[a]) + carried[a]).astype(BF16)
        qg_ref[0, b, lanes] = (dot_nn(lower, k) + carried[b]).astype(BF16)
        table = jnp.concatenate([diagonal_t, below_t], axis=1)
        for x, y, z, ref in ((v, g, q, kl_ref), (k, q, g, vl_ref)):
            first = (dot_nt(x[a], y) * table).astype(BF16)
            second = (dot_nt(x[b], y[b]) * diagonal_t).astype(BF16)
            ref[a, lanes] = dot_nn(first, z)
            ref[b, lanes] = dot_nn(second, z[b])


def final_kernel(per_step, slab, rows, index_ref, r_ref, k_ref, v_ref, kl_ref, vl_ref, kg_ref, vg_ref, gain_ref):
    step = pl.program_id(0)
    pieces = LANES // rows
    gains = jnp.zeros(gain_ref.shape, F32)
    for i in range(per_step):
        rate = rate_of(index_ref[step * per_step + i], slab)
        lanes = slice(i * LANES, (i + 1) * LANES)
        to_next = row_powers(rate, float(slab), -1.0, slab)
        back = jnp.concatenate([r_ref[i * pieces + p, :rows] for p in range(pieces)], axis=0).astype(BF16)
        kg_ref[0, :, lanes] = (kl_ref[:, lanes] + dot_nt(head(v_ref, i), back) * to_next).astype(BF16)
        vg_ref[0, :, lanes] = (vl_ref[:, lanes] + dot_nn(head(k_ref, i), back) * to_next).astype(BF16)
        for p in range(pieces):
            gains += r_ref[i * pieces + p, rows:]

    @pl.when(step == 0)
    def _():
        gain_ref[...] = gains

    @pl.when(step != 0)
    def _():
        gain_ref[...] += gains


def on_device(query_rows, key_rows, value_rows, norm_gain, cotangent, loss_mask, importance, advantage, lengths, decay_index):
    _, slab, features = query_rows.shape
    heads = decay_index.shape[0]
    slabs = lax.axis_size("seq")
    place = lax.axis_index("seq")
    rows = heads * LANES // slabs
    total_features = float(features * lax.axis_size("head"))
    per_step = 2
    steps = heads // per_step
    wide = per_step * LANES
    gain_row = norm_gain.reshape(1, features)

    smem = pl.BlockSpec(memory_space=pltpu.SMEM)
    token = pl.BlockSpec((1, slab, wide), lambda i: (0, 0, i))
    flat = pl.BlockSpec((slab, wide), lambda i: (0, i))
    column = pl.BlockSpec((slab, LANES), lambda i: (0, 0))
    gain_spec = pl.BlockSpec((1, wide), lambda i: (0, i))
    state = pl.BlockSpec((per_step, LANES, LANES), lambda i: (i, 0, 0))
    token_f32 = jax.ShapeDtypeStruct((slab, features), F32)
    column_f32 = jax.ShapeDtypeStruct((slab, LANES), F32)
    token_out = jax.ShapeDtypeStruct(query_rows.shape, BF16)
    state_f32 = jax.ShapeDtypeStruct((heads, LANES, LANES), F32)
    params = pltpu.CompilerParams(dimension_semantics=("arbitrary",))

    def over_slabs(pieces):
        return lax.all_to_all(pieces, "seq", 0, 0, tiled=True)

    own_head = lax.dynamic_slice(decay_index, (place * rows // LANES,), (1,))

    state_local = pl.pallas_call(
        functools.partial(state_kernel, per_step, slab),
        grid=(steps,),
        in_specs=[smem, token, token],
        out_specs=state,
        out_shape=state_f32,
        compiler_params=params,
        name="state_local",
    )(decay_index, key_rows, value_rows)
    sent = over_slabs(state_local.reshape(slabs, rows, LANES))

    local_out, weight = pl.pallas_call(
        functools.partial(local_kernel, per_step, slab, slab * slabs),
        grid=(steps,),
        in_specs=[smem, smem, smem, smem, token, token, token]
        + [pl.BlockSpec((1, slab), lambda i: (0, 0))] * 2,
        out_specs=[flat, column],
        out_shape=[token_f32, column_f32],
        compiler_params=params,
        name="local_attention",
    )(decay_index, place.reshape(1), lengths, advantage, query_rows, key_rows, value_rows, loss_mask, importance)

    piece_f32 = jax.ShapeDtypeStruct((slabs, rows, LANES), F32)
    before = pl.pallas_call(
        functools.partial(scan_kernel, slabs, slab, False),
        in_specs=[smem, pl.BlockSpec(memory_space=pltpu.VMEM)],
        out_specs=pl.BlockSpec(memory_space=pltpu.VMEM),
        out_shape=piece_f32,
        name="prefix",
    )(own_head, sent)
    state_in = over_slabs(before).reshape(heads, LANES, LANES)

    groups = lax.axis_size("head")
    stat_rows = 2 * slab // LANES
    outputs, stats = pl.pallas_call(
        functools.partial(output_kernel, per_step, slab),
        grid=(steps,),
        in_specs=[smem, token, state, flat, token, column, gain_spec],
        out_specs=[flat, pl.BlockSpec((groups, stat_rows, LANES), lambda i: (0, 0, 0))],
        out_shape=[token_f32, jax.ShapeDtypeStruct((groups, stat_rows, LANES), F32)],
        scratch_shapes=[pltpu.VMEM((slab, LANES), F32)] * 2,
        compiler_params=params,
        name="outputs",
    )(decay_index, query_rows, state_in, local_out, cotangent, weight, gain_row)
    stats = lax.all_to_all(stats, "head", 0, 0, tiled=True)

    grad_out, return_local, gain_part, inverse, _ = pl.pallas_call(
        functools.partial(grad_kernel, per_step, slab, total_features),
        grid=(steps,),
        in_specs=[
            smem, pl.BlockSpec((groups, stat_rows, LANES), lambda i: (0, 0, 0)), token, flat, token, column, gain_spec
        ],
        out_specs=[flat, state, pl.BlockSpec((heads, LANES), lambda i: (0, 0)), column, column],
        out_shape=[
            jax.ShapeDtypeStruct((slab, features), BF16), state_f32, jax.ShapeDtypeStruct((heads, LANES), F32),
            column_f32, column_f32,
        ],
        scratch_shapes=[pltpu.VMEM((slab, LANES), F32)] * 2,
        compiler_params=params,
        name="output_grad",
    )(decay_index, stats, query_rows, outputs, cotangent, weight, gain_row)
    returned = over_slabs(return_local.reshape(slabs, rows, LANES))
    gain_part = lax.psum(gain_part, "dp")

    mixed, query_grad, key_local, value_local = pl.pallas_call(
        functools.partial(backward_kernel, per_step, slab),
        grid=(steps,),
        in_specs=[smem, token, token, token, flat, state, flat, column, gain_spec],
        out_specs=[token, token, flat, flat],
        out_shape=[token_out, token_out, token_f32, token_f32],
        compiler_params=params,
        name="local_grads",
    )(decay_index, query_rows, key_rows, value_rows, grad_out, state_in, outputs, inverse, gain_row)

    after = pl.pallas_call(
        functools.partial(scan_gain_kernel, slabs, slab),
        in_specs=[smem, pl.BlockSpec(memory_space=pltpu.VMEM), pl.BlockSpec(memory_space=pltpu.VMEM)],
        out_specs=pl.BlockSpec(memory_space=pltpu.VMEM),
        out_shape=jax.ShapeDtypeStruct((slabs, rows + heads, LANES), F32),
        name="suffix",
    )(own_head, returned, gain_part)
    return_in = over_slabs(after)

    pieces = LANES // rows
    key_grad, value_grad, gain_grad = pl.pallas_call(
        functools.partial(final_kernel, per_step, slab, rows),
        grid=(steps,),
        in_specs=[
            smem, pl.BlockSpec((per_step * pieces, rows + heads, LANES), lambda i: (i, 0, 0)), token, token, flat, flat
        ],
        out_specs=[token, token, pl.BlockSpec((heads, LANES), lambda i: (0, 0))],
        out_shape=[token_out, token_out, jax.ShapeDtypeStruct((heads, LANES), F32)],
        compiler_params=params,
        name="final_grads",
    )(decay_index, return_in, key_rows, value_rows, key_local, value_local)
    return (mixed, query_grad, key_grad, value_grad, gain_grad.reshape(features))


def solution(mesh):
    tokens = P("dp", "seq", "head")
    return jax.shard_map(
        on_device,
        mesh=mesh,
        in_specs=(
            tokens, tokens, tokens, P("head"), tokens, P("dp", "seq"), P("dp", "seq"), P("dp"), P("dp"), P("head"),
        ),
        out_specs=(tokens, tokens, tokens, tokens, P("head")),
        check_vma=False,
    )
```

```python
import functools

import jax
import jax.numpy as jnp
from jax import lax
from jax.experimental import pallas as pl
from jax.experimental.pallas import tpu as pltpu
from jax.sharding import PartitionSpec as P

clip_high = 1.28
epsilon = 1e-06
F32 = jnp.float32
BF16 = jnp.bfloat16
LANES = 128
HALF = 256


def dot_nn(a, b):
    return lax.dot_general(a, b, (((1,), (0,)), ((), ())), preferred_element_type=F32)


def dot_nt(a, b):
    return lax.dot_general(a, b, (((1,), (1,)), ((), ())), preferred_element_type=F32)


def dot_tn(a, b):
    return lax.dot_general(a, b, (((0,), (0,)), ((), ())), preferred_element_type=F32)


def rate_of(index, slab):
    return (16.0 / slab) * jnp.exp2(jnp.full((1, LANES), -index.astype(F32), F32))


def row_powers(rate, first, step, rows):
    at = lax.broadcasted_iota(jnp.int32, (LANES, LANES), 0).astype(F32)
    powers = jnp.exp2(-rate * (first + step * at))
    parts = [powers] + [powers * jnp.exp2(-rate * (step * b)) for b in range(LANES, rows, LANES)]
    return jnp.concatenate(parts, axis=0) if len(parts) > 1 else powers


def decay_blocks(rate, transposed):
    rate2 = jnp.concatenate([rate] * (HALF // LANES), axis=1)
    rows = lax.broadcasted_iota(jnp.int32, (HALF, HALF), 0)
    cols = lax.broadcasted_iota(jnp.int32, (HALF, HALF), 1)
    lag = (cols - rows if transposed else rows - cols).astype(F32)
    powers = jnp.exp2(-rate2 * lag)
    return jnp.where(lag >= 0, powers, 0.0), powers * jnp.exp2(-rate2 * float(HALF))


def head(ref, i):
    return ref[0, :, i * LANES : (i + 1) * LANES]


def from_vmem(x):
    return pltpu.with_memory_space_constraint(x, pltpu.VMEM)


def from_hbm(x):
    return pltpu.with_memory_space_constraint(x, pltpu.HBM)


class Copies:
    def __init__(self, semaphores):
        self.semaphores = semaphores
        self.used = 0

    def start(self, source, target):
        copy = pltpu.make_async_copy(source, target, self.semaphores.at[self.used])
        self.used += 1
        copy.start()
        return copy


def wait_all(copies):
    for copy in copies:
        copy.wait()


def lanes_of(first, count=1):
    return slice(first * LANES, (first + count) * LANES)


def column(row):
    return jnp.broadcast_to(row, (LANES, LANES)).T


def state_kernel(heads, group, slab, index_hbm, k_hbm, v_hbm, out_hbm, index, k, v, out, semaphores):
    copies = Copies(semaphores)
    index_copy = copies.start(index_hbm, index)
    loads = []
    for first in range(0, heads, group):
        lanes = lanes_of(first, group)
        loads.append([copies.start(x.at[0, :, lanes], y.at[:, lanes]) for x, y in ((k_hbm, k), (v_hbm, v))])
    stores = []
    index_copy.wait()
    for first in range(0, heads, group):
        wait_all(loads[first // group])
        for h in range(first, first + group):
            rate = rate_of(index[h], slab)
            decayed = k[:, lanes_of(h)].astype(F32) * row_powers(rate, slab - 1.0, -1.0, slab)
            out[h] = dot_tn(decayed.astype(BF16), v[:, lanes_of(h)])
        part = slice(first, first + group)
        stores.append(copies.start(out.at[part], out_hbm.at[part]))
    wait_all(stores)


def scan_kernel(slabs, slab, reverse, group, index_ref, place_ref, x_ref, *refs):
    extra, (out_hbm, out, semaphores) = refs[:-3], refs[-3:]
    copies = Copies(semaphores)
    rows = x_ref.shape[1]
    rate = rate_of(index_ref[(place_ref[0] * rows) // LANES], slab)
    factor = jnp.exp2(-rate * float(slab))
    running = jnp.zeros(x_ref.shape[1:], F32)
    order = list(reversed(range(slabs))) if reverse else list(range(slabs))
    stores = []
    for at in range(0, slabs, group):
        for j in order[at : at + group]:
            out[j, :rows] = running
            if extra:
                out[j, rows:] = extra[0][...]
            running = factor * running + x_ref[j]
        part = slice(min(order[at : at + group]), max(order[at : at + group]) + 1)
        stores.append(copies.start(out.at[part], out_hbm.at[part]))
    wait_all(stores)


def local_kernel(
    per_step, slab, total, index_ref, place_ref, length_ref, advantage_ref, q_ref, k_ref, v_ref, mask_ref, imp_ref,
    out_ref, weight_ref,
):
    @pl.when(pl.program_id(0) == 0)
    def _():
        at = place_ref[0] * slab + lax.broadcasted_iota(jnp.int32, (1, slab), 1)
        inside = (at < length_ref[0]).astype(F32)
        length = jnp.full((1, slab), length_ref[0].astype(F32), F32)
        weight = mask_ref[...].astype(F32) * inside * jnp.minimum(imp_ref[...], clip_high)
        weight = weight * advantage_ref[0] * (float(total) / length)
        for b in range(slab // LANES):
            weight_ref[b : b + 1, :] = weight[:, lanes_of(b)]

    for i in range(per_step):
        rate = rate_of(index_ref[pl.program_id(0) * per_step + i], slab)
        diagonal, below = decay_blocks(rate, False)
        q, k, v = head(q_ref, i), head(k_ref, i), head(v_ref, i)
        lanes = lanes_of(i)
        for r in range(slab // HALF):
            scores = dot_nt(q[r * HALF : (r + 1) * HALF], k[: (r + 1) * HALF])
            table = diagonal if r == 0 else jnp.concatenate([below, diagonal], axis=1)
            probs = (scores * table).astype(BF16)
            out_ref[r * HALF : (r + 1) * HALF, lanes] = dot_nn(probs, v[: (r + 1) * HALF])


def output_kernel(
    heads, slab, index_hbm, q_hbm, s_ref, local, c_hbm, weight_ref, gain_hbm, out, q, grad_n, stat_ref,
    index, gain, c, s, semaphores,
):
    copies = Copies(semaphores)
    small = [copies.start(index_hbm, index), copies.start(gain_hbm, gain)]
    loads = []
    for b in range(slab // LANES):
        rows = lanes_of(b)
        loads.append([
            copies.start(q_hbm.at[0, rows], q.at[rows]),
            copies.start(c_hbm.at[0, rows], c.at[rows]),
        ])
    for h in range(heads):
        s[h] = s_ref[h].astype(BF16)
    wait_all(small)
    square_rows, cross_rows = [], []
    for b in range(slab // LANES):
        rows = lanes_of(b)
        weight = column(weight_ref[b : b + 1, :])
        squares = jnp.zeros((LANES, LANES), F32)
        crosses = jnp.zeros((LANES, LANES), F32)
        wait_all(loads[b])
        for h in range(heads):
            rate = rate_of(index[h], slab)
            lanes = lanes_of(h)
            carried = dot_nn(q[rows, lanes], s[h])
            o = local[rows, lanes] + carried * row_powers(rate, b * LANES + 1.0, 1.0, LANES)
            out[rows, lanes] = o
            squares += o * o
            grad = c[rows, lanes].astype(F32) * weight * gain[:, lanes]
            grad_n[rows, lanes] = grad
            crosses += grad * o
        square_rows.append(jnp.sum(squares.T, axis=0, keepdims=True))
        cross_rows.append(jnp.sum(crosses.T, axis=0, keepdims=True))
    stats = jnp.concatenate(square_rows + cross_rows, axis=0)
    for d in range(stat_ref.shape[0]):
        stat_ref[d] = stats


def grad_kernel(
    heads, group, slab, features, index_hbm, stat_ref, q, o, grad_n,
    g_hbm, o_hbm, ret_hbm, inv_ref, index, g, ret, inv_col, mean_col, semaphores,
):
    copies = Copies(semaphores)
    index_copy = copies.start(index_hbm, index)
    stores = [copies.start(o, o_hbm)]
    stats = jnp.sum(stat_ref[...], axis=0)
    blocks = slab // LANES
    inverse = lax.rsqrt(stats[:blocks] / features + epsilon)
    mean = stats[blocks : 2 * blocks] * inverse / features * (inverse * inverse)
    inv_ref[...] = inverse
    for b in range(blocks):
        rows = lanes_of(b)
        inv_col[rows, :] = column(inverse[b : b + 1])
        mean_col[rows, :] = column(mean[b : b + 1])
    index_copy.wait()
    for first in range(0, heads, group):
        for h in range(first, first + group):
            rate = rate_of(index[h], slab)
            lanes = lanes_of(h)
            grad_out = (inv_col[...] * grad_n[:, lanes] - o[:, lanes] * mean_col[...]).astype(BF16)
            g[:, lanes] = grad_out
            decayed = q[:, lanes].astype(F32) * row_powers(rate, 0.0, 1.0, slab)
            ret[h] = dot_tn(decayed.astype(BF16), grad_out)
        part = slice(first, first + group)
        lanes = lanes_of(first, group)
        stores.append(copies.start(ret.at[part], ret_hbm.at[part]))
        stores.append(copies.start(g.at[:, lanes], g_hbm.at[:, lanes]))
    wait_all(stores)


def query_grad_kernel(
    per_step, slab, index_ref, k_ref, v_ref, g_ref, s_ref, o_ref, c_ref, inv_ref, weight_ref,
    qg_ref, gain_out_ref, scale_col,
):
    step = pl.program_id(0)

    @pl.when(step == 0)
    def _():
        for b in range(slab // LANES):
            scale_col[lanes_of(b), :] = column(inv_ref[b : b + 1, :] * weight_ref[b : b + 1, :])

    for i in range(per_step):
        rate = rate_of(index_ref[step * per_step + i], slab)
        lanes = lanes_of(i)
        products = head(c_ref, i).astype(F32) * (o_ref[:, lanes] * scale_col[...])
        gain_out_ref[pl.ds(step * per_step + i, 1), :] = jnp.sum(products, axis=0, keepdims=True)
        k, v, g = head(k_ref, i), head(v_ref, i), g_ref[:, lanes]
        diagonal, below = decay_blocks(rate, False)
        carried = dot_nt(g, s_ref[i].astype(BF16)) * row_powers(rate, 1.0, 1.0, slab)
        a, b = slice(0, HALF), slice(HALF, 2 * HALF)
        upper = (dot_nt(g[a], v[a]) * diagonal).astype(BF16)
        lower = (dot_nt(g[b], v) * jnp.concatenate([below, diagonal], axis=1)).astype(BF16)
        qg_ref[0, a, lanes] = (dot_nn(upper, k[a]) + carried[a]).astype(BF16)
        qg_ref[0, b, lanes] = (dot_nn(lower, k) + carried[b]).astype(BF16)


def key_value_kernel(
    per_step, slab, index_ref, q_ref, k_ref, v_ref, g_ref, o_ref, inv_ref, gain_ref, mixed_ref, kl_ref, vl_ref, inv_col
):
    @pl.when(pl.program_id(0) == 0)
    def _():
        for b in range(slab // LANES):
            inv_col[lanes_of(b), :] = column(inv_ref[b : b + 1, :])

    for i in range(per_step):
        mixed_ref[0, :, lanes_of(i)] = (o_ref[:, lanes_of(i)] * inv_col[...] * gain_ref[:, lanes_of(i)]).astype(BF16)
        rate = rate_of(index_ref[pl.program_id(0) * per_step + i], slab)
        lanes = lanes_of(i)
        q, k, v, g = head(q_ref, i), head(k_ref, i), head(v_ref, i), g_ref[:, lanes]
        diagonal, below = decay_blocks(rate, True)
        a, b = slice(0, HALF), slice(HALF, 2 * HALF)
        table = jnp.concatenate([diagonal, below], axis=1)
        for x, y, z, ref in ((v, g, q, kl_ref), (k, q, g, vl_ref)):
            first = (dot_nt(x[a], y) * table).astype(BF16)
            second = (dot_nt(x[b], y[b]) * diagonal).astype(BF16)
            ref[a, lanes] = dot_nn(first, z).astype(BF16)
            ref[b, lanes] = dot_nn(second, z[b]).astype(BF16)


def final_kernel(
    heads, group, slab, size, index_hbm, r_ref, k_hbm, v_hbm, kl, vl, kg_hbm, vg_hbm, index, k, v, kg, vg, semaphores
):
    copies = Copies(semaphores)
    index_copy = copies.start(index_hbm, index)
    loads = []
    for first in range(0, heads, group):
        lanes = lanes_of(first, group)
        loads.append([copies.start(x.at[0, :, lanes], y.at[:, lanes]) for x, y in ((k_hbm, k), (v_hbm, v))])
    pieces = LANES // size
    index_copy.wait()
    stores = []
    for first in range(0, heads, group):
        wait_all(loads[first // group])
        for h in range(first, first + group):
            lanes = lanes_of(h)
            to_next = row_powers(rate_of(index[h], slab), float(slab), -1.0, slab)
            back = jnp.concatenate([r_ref[h * pieces + p, :size] for p in range(pieces)], axis=0).astype(BF16)
            kg[:, lanes] = (kl[:, lanes].astype(F32) + dot_nt(v[:, lanes], back) * to_next).astype(BF16)
            vg[:, lanes] = (vl[:, lanes].astype(F32) + dot_nn(k[:, lanes], back) * to_next).astype(BF16)
        lanes = lanes_of(first, group)
        stores += [copies.start(x.at[:, lanes], y.at[0, :, lanes]) for x, y in ((kg, kg_hbm), (vg, vg_hbm))]
    wait_all(stores)


def on_device(query_rows, key_rows, value_rows, norm_gain, cotangent, loss_mask, importance, advantage, lengths, decay_index):
    _, slab, features = query_rows.shape
    heads = decay_index.shape[0]
    slabs = lax.axis_size("seq")
    place = lax.axis_index("seq").reshape(1)
    size = heads * LANES // slabs
    total_features = float(features * lax.axis_size("head"))
    per_step = 2
    steps = heads // per_step
    wide = per_step * LANES
    blocks = slab // LANES
    gain_row = from_hbm(norm_gain.reshape(1, features))
    decay_hbm, query, key, value, upstream = map(from_hbm, (decay_index, query_rows, key_rows, value_rows, cotangent))

    smem = pl.BlockSpec(memory_space=pltpu.SMEM)
    vmem = pl.BlockSpec(memory_space=pltpu.VMEM)
    anywhere = pl.BlockSpec(memory_space=pl.ANY)
    token = pl.BlockSpec((1, slab, wide), lambda i: (0, 0, i))
    flat = pl.BlockSpec((slab, wide), lambda i: (0, i))
    gain_spec = pl.BlockSpec((1, wide), lambda i: (0, i))
    state = pl.BlockSpec((per_step, LANES, LANES), lambda i: (i, 0, 0))
    token_row = pl.BlockSpec((blocks, LANES), lambda i: (0, 0))
    gain_out = pl.BlockSpec((heads, LANES), lambda i: (0, 0))
    token_f32 = pltpu.HBM((slab, features), F32)
    token_out = pltpu.HBM(query_rows.shape, BF16)
    state_out = pltpu.HBM((heads, LANES, LANES), F32)
    row_out = jax.ShapeDtypeStruct((blocks, LANES), F32)
    gain_f32 = jax.ShapeDtypeStruct((heads, LANES), F32)
    params = pltpu.CompilerParams(vmem_limit_bytes=24 * 1024 * 1024)

    def held(dtype):
        return pltpu.VMEM((slab, features), dtype)

    def semaphores(count):
        return pltpu.SemaphoreType.DMA((count,))

    index_held = pltpu.SMEM((heads,), jnp.int32)
    gain_held = pltpu.VMEM((1, features), F32)
    state_held = pltpu.VMEM((heads, LANES, LANES), F32)
    state_half = pltpu.VMEM((heads, LANES, LANES), BF16)
    columns = pltpu.VMEM((slab, LANES), F32)

    def over_slabs(pieces):
        return lax.all_to_all(pieces, "seq", 0, 0, tiled=True)

    group = 2
    state_local = pl.pallas_call(
        functools.partial(state_kernel, heads, group, slab),
        in_specs=[anywhere] * 3,
        out_specs=anywhere,
        out_shape=state_out,
        scratch_shapes=[index_held, held(BF16), held(BF16), state_held, semaphores(1 + 3 * heads // group)],
        compiler_params=params,
        name="state_local",
    )(decay_hbm, key, value)
    sent = over_slabs(state_local.reshape(slabs, size, LANES))

    local_out, weight = pl.pallas_call(
        functools.partial(local_kernel, per_step, slab, slab * slabs),
        grid=(steps,),
        in_specs=[smem, smem, smem, smem, token, token, token]
        + [pl.BlockSpec((1, slab), lambda i: (0, 0))] * 2,
        out_specs=[flat, token_row],
        out_shape=[pltpu.VMEM((slab, features), F32), row_out],
        compiler_params=params,
        name="local_attention",
    )(decay_index, place, lengths, advantage, query, key, value, loss_mask, importance)
    local_out = from_vmem(local_out)

    def scan(reverse, pieces, extra, name):
        shape = (slabs, size + (heads if extra else 0), LANES)
        return pl.pallas_call(
            functools.partial(scan_kernel, slabs, slab, reverse, 4),
            in_specs=[smem, smem, vmem] + [vmem] * len(extra),
            out_specs=anywhere,
            out_shape=pltpu.HBM(shape, F32),
            scratch_shapes=[pltpu.VMEM(shape, F32), semaphores(slabs // 4)],
            compiler_params=params,
            name=name,
        )(decay_index, place, pieces, *extra)

    state_in = over_slabs(scan(False, sent, (), "prefix")).reshape(heads, LANES, LANES)

    groups = lax.axis_size("head")
    outputs, query_held, grad_n, stats = pl.pallas_call(
        functools.partial(output_kernel, heads, slab),
        in_specs=[anywhere, anywhere, vmem, vmem, anywhere, vmem, anywhere],
        out_specs=[vmem] * 4,
        out_shape=[held(F32), held(BF16), held(F32), jax.ShapeDtypeStruct((groups, 2 * blocks, LANES), F32)],
        scratch_shapes=[index_held, gain_held, held(BF16), state_half, semaphores(2 + 2 * blocks)],
        compiler_params=params,
        name="outputs",
    )(decay_hbm, query, state_in, local_out, upstream, weight, gain_row)
    stats = lax.all_to_all(stats, "head", 0, 0, tiled=True)

    grad_out, outputs, return_local, inverse = pl.pallas_call(
        functools.partial(grad_kernel, heads, group, slab, total_features),
        in_specs=[anywhere, vmem, vmem, vmem, vmem],
        out_specs=[anywhere, anywhere, anywhere, vmem],
        out_shape=[pltpu.HBM((slab, features), BF16), token_f32, state_out, row_out],
        scratch_shapes=[
            index_held, held(BF16), state_held, columns, columns, semaphores(2 + 2 * heads // group)
        ],
        compiler_params=params,
        name="output_grad",
    )(decay_hbm, stats, from_vmem(query_held), from_vmem(outputs), from_vmem(grad_n))
    grad_out, outputs = from_hbm(grad_out), from_hbm(outputs)
    returned = over_slabs(return_local.reshape(slabs, size, LANES))

    query_grad, gain_part = pl.pallas_call(
        functools.partial(query_grad_kernel, per_step, slab),
        grid=(steps,),
        in_specs=[smem, token, token, flat, state, flat, token, token_row, token_row],
        out_specs=[token, gain_out],
        out_shape=[token_out, gain_f32],
        scratch_shapes=[columns],
        compiler_params=params,
        name="query_grads",
    )(decay_index, key, value, grad_out, state_in, outputs, upstream, inverse, weight)
    return_in = over_slabs(scan(True, returned, (gain_part,), "suffix"))

    mixed, key_local, value_local = pl.pallas_call(
        functools.partial(key_value_kernel, per_step, slab),
        grid=(steps,),
        in_specs=[smem, token, token, token, flat, flat, token_row, gain_spec],
        out_specs=[token, flat, flat],
        out_shape=[token_out, held(BF16), held(BF16)],
        scratch_shapes=[columns],
        compiler_params=params,
        name="key_value_grads",
    )(decay_index, query, key, value, grad_out, outputs, inverse, gain_row)

    return_in, key_local, value_local = lax.optimization_barrier((return_in, key_local, value_local))
    gain_sum = jnp.sum(return_in[:, size:], axis=0)
    other_sum = lax.ppermute(gain_sum, "dp", [(i, 1 - i) for i in range(2)])
    key_grad, value_grad = pl.pallas_call(
        functools.partial(final_kernel, heads, group, slab, size),
        in_specs=[anywhere, vmem, anywhere, anywhere, vmem, vmem],
        out_specs=[anywhere, anywhere],
        out_shape=[token_out, token_out],
        scratch_shapes=[index_held] + [held(BF16)] * 4 + [semaphores(1 + 4 * heads // group)],
        compiler_params=params,
        name="final_grads",
    )(decay_hbm, return_in, key, value, from_vmem(key_local), from_vmem(value_local))
    gain_grad = (gain_sum + other_sum).reshape(features)
    return (mixed, query_grad, key_grad, value_grad, gain_grad)


def solution(mesh):
    tokens = P("dp", "seq", "head")
    return jax.shard_map(
        on_device,
        mesh=mesh,
        in_specs=(
            tokens, tokens, tokens, P("head"), tokens, P("dp", "seq"), P("dp", "seq"), P("dp"), P("dp"), P("head"),
        ),
        out_specs=(tokens, tokens, tokens, tokens, P("head")),
        check_vma=False,
    )
```

```python
import functools

import jax
import jax.numpy as jnp
from jax import lax
from jax.experimental import pallas as pl
from jax.experimental.pallas import tpu as pltpu
from jax.sharding import PartitionSpec as P

clip_high = 1.28
epsilon = 1e-06
F32 = jnp.float32
BF16 = jnp.bfloat16
LANES = 128
HALF = 256


def dot_nn(a, b):
    return lax.dot_general(a, b, (((1,), (0,)), ((), ())), preferred_element_type=F32)


def dot_nt(a, b):
    return lax.dot_general(a, b, (((1,), (1,)), ((), ())), preferred_element_type=F32)


def dot_tn(a, b):
    return lax.dot_general(a, b, (((0,), (0,)), ((), ())), preferred_element_type=F32)


def rate_of(index, slab):
    return (16.0 / slab) * jnp.exp2(jnp.full((1, LANES), -index.astype(F32), F32))


def row_powers(rate, first, step, rows):
    at = lax.broadcasted_iota(jnp.int32, (LANES, LANES), 0).astype(F32)
    powers = jnp.exp2(-rate * (first + step * at))
    parts = [powers] + [powers * jnp.exp2(-rate * (step * b)) for b in range(LANES, rows, LANES)]
    return jnp.concatenate(parts, axis=0) if len(parts) > 1 else powers


def decay_blocks(rate, transposed):
    rate2 = jnp.concatenate([rate] * (HALF // LANES), axis=1)
    rows = lax.broadcasted_iota(jnp.int32, (HALF, HALF), 0)
    cols = lax.broadcasted_iota(jnp.int32, (HALF, HALF), 1)
    lag = (cols - rows if transposed else rows - cols).astype(F32)
    powers = jnp.exp2(-rate2 * lag)
    return jnp.where(lag >= 0, powers, 0.0), powers * jnp.exp2(-rate2 * float(HALF))


def head(ref, i):
    return ref[0, :, i * LANES : (i + 1) * LANES]


def from_vmem(x):
    return pltpu.with_memory_space_constraint(x, pltpu.VMEM)


def from_hbm(x):
    return pltpu.with_memory_space_constraint(x, pltpu.HBM)


class Copies:
    def __init__(self, semaphores):
        self.semaphores = semaphores
        self.used = 0

    def start(self, source, target):
        copy = pltpu.make_async_copy(source, target, self.semaphores.at[self.used])
        self.used += 1
        copy.start()
        return copy


def wait_all(copies):
    for copy in copies:
        copy.wait()


def lanes_of(first, count=1):
    return slice(first * LANES, (first + count) * LANES)


def column(row):
    return jnp.broadcast_to(row, (LANES, LANES)).T


def state_kernel(heads, slab, index_hbm, k_hbm, v_hbm, out_hbm, index, k, v, out, semaphores):
    copies = Copies(semaphores)
    index_copy = copies.start(index_hbm, index)
    spans = [slice(at, at + HALF) for at in range(0, slab, HALF)]
    loads = [[copies.start(x.at[0, rows], y.at[rows]) for x, y in ((k_hbm, k), (v_hbm, v))] for rows in spans]
    stores = []
    index_copy.wait()
    for rows, load in zip(spans, loads):
        wait_all(load)
        for h in range(heads):
            powers = row_powers(rate_of(index[h], slab), slab - 1.0 - rows.start, -1.0, HALF)
            decayed = (k[rows, lanes_of(h)].astype(F32) * powers).astype(BF16)
            term = dot_tn(decayed, v[rows, lanes_of(h)])
            out[h] = term if rows.start == 0 else out[h] + term
            if rows.stop == slab and h % 4 == 3:
                part = slice(h - 3, h + 1)
                stores.append(copies.start(out.at[part], out_hbm.at[part]))
    wait_all(stores)


def scan_kernel(slabs, slab, size, reverse, group, index_ref, place_ref, x_ref, out_hbm, *refs):
    extra, (out, semaphores) = refs[:-2], refs[-2:]
    copies = Copies(semaphores)
    rate = rate_of(index_ref[(place_ref[0] * size) // LANES], slab)
    factor = jnp.exp2(-rate * float(slab))
    running = jnp.zeros((size, LANES), F32)
    order = list(reversed(range(slabs))) if reverse else list(range(slabs))
    stores = []
    for at in range(0, slabs, group):
        for j in order[at : at + group]:
            out[j] = running
            running = factor * running + x_ref[j, :size]
        part = slice(min(order[at : at + group]), max(order[at : at + group]) + 1)
        stores.append(copies.start(out.at[part], out_hbm.at[part]))
    if extra:
        total = x_ref[0, size:]
        for j in range(1, slabs):
            total += x_ref[j, size:]
        extra[0][...] = total
    wait_all(stores)


def local_kernel(
    per_step, slab, total, index_ref, place_ref, length_ref, advantage_ref, q_ref, k_ref, v_ref, mask_ref, imp_ref,
    out_ref, weight_ref,
):
    @pl.when(pl.program_id(0) == 0)
    def _():
        at = place_ref[0] * slab + lax.broadcasted_iota(jnp.int32, (1, slab), 1)
        inside = (at < length_ref[0]).astype(F32)
        length = jnp.full((1, slab), length_ref[0].astype(F32), F32)
        weight = mask_ref[...].astype(F32) * inside * jnp.minimum(imp_ref[...], clip_high)
        weight = weight * advantage_ref[0] * (float(total) / length)
        for b in range(slab // LANES):
            weight_ref[b : b + 1, :] = weight[:, lanes_of(b)]

    for i in range(per_step):
        rate = rate_of(index_ref[pl.program_id(0) * per_step + i], slab)
        diagonal, below = decay_blocks(rate, False)
        q, k, v = head(q_ref, i), head(k_ref, i), head(v_ref, i)
        lanes = lanes_of(i)
        for r in range(slab // HALF):
            scores = dot_nt(q[r * HALF : (r + 1) * HALF], k[: (r + 1) * HALF])
            table = diagonal if r == 0 else jnp.concatenate([below, diagonal], axis=1)
            probs = (scores * table).astype(BF16)
            out_ref[r * HALF : (r + 1) * HALF, lanes] = dot_nn(probs, v[: (r + 1) * HALF])


def output_kernel(
    heads, slab, index_hbm, q_hbm, s_ref, local, c_hbm, weight_ref, gain_hbm, out, q, grad_y, stat_ref,
    index, gain, c, s, semaphores,
):
    copies = Copies(semaphores)
    small = [copies.start(index_hbm, index), copies.start(gain_hbm, gain)]
    loads = []
    span = HALF // LANES
    for b in range(0, slab // LANES, span):
        rows = lanes_of(b, span)
        loads.append([
            copies.start(q_hbm.at[0, rows], q.at[rows]),
            copies.start(c_hbm.at[0, rows], c.at[rows]),
        ])
    for h in range(heads):
        s[h] = s_ref[h].astype(BF16)
    wait_all(small)
    square_rows, cross_rows = [], []
    for b in range(0, slab // LANES, span):
        rows = lanes_of(b, span)
        weight = jnp.concatenate([column(weight_ref[x : x + 1, :]) for x in range(b, b + span)], axis=0)
        squares = jnp.zeros((HALF, LANES), F32)
        crosses = jnp.zeros((HALF, LANES), F32)
        wait_all(loads[b // span])
        for h in range(heads):
            rate = rate_of(index[h], slab)
            lanes = lanes_of(h)
            carried = dot_nn(q[rows, lanes], s[h])
            o = local[rows, lanes] + carried * row_powers(rate, b * LANES + 1.0, 1.0, HALF)
            out[rows, lanes] = o
            squares += o * o
            grad = c[rows, lanes].astype(F32) * weight
            grad_y[rows, lanes] = grad
            crosses += (grad * gain[:, lanes]) * o
        for x in range(span):
            square_rows.append(jnp.sum(squares[lanes_of(x)].T, axis=0, keepdims=True))
            cross_rows.append(jnp.sum(crosses[lanes_of(x)].T, axis=0, keepdims=True))
    stats = jnp.concatenate(square_rows + cross_rows, axis=0)
    for d in range(stat_ref.shape[0]):
        stat_ref[d] = stats


def grad_kernel(
    heads, group, slab, features, size, index_hbm, stat_ref, q, o, grad_y, gain_hbm,
    g_hbm, o_hbm, ret_hbm, inv_ref, index, gain, g, ret, inv_col, mean_col, semaphores,
):
    copies = Copies(semaphores)
    small = [copies.start(index_hbm, index), copies.start(gain_hbm, gain)]
    stores = [copies.start(o, o_hbm)]
    stats = jnp.sum(stat_ref[...], axis=0)
    blocks = slab // LANES
    inverse = lax.rsqrt(stats[:blocks] / features + epsilon)
    mean = stats[blocks : 2 * blocks] * inverse / features
    inv_ref[...] = inverse
    for b in range(blocks):
        rows = lanes_of(b)
        inv_col[rows, :] = column(inverse[b : b + 1])
        mean_col[rows, :] = column(mean[b : b + 1])
    wait_all(small)
    pieces = LANES // size
    gain_rows = []
    for first in range(0, heads, group):
        for h in range(first, first + group):
            rate = rate_of(index[h], slab)
            lanes = lanes_of(h)
            normed = o[:, lanes] * inv_col[...]
            gain_rows.append(jnp.sum(grad_y[:, lanes] * normed, axis=0, keepdims=True))
            grad_n = grad_y[:, lanes] * gain[:, lanes]
            grad_out = (inv_col[...] * (grad_n - normed * mean_col[...])).astype(BF16)
            g[:, lanes] = grad_out
            decayed = q[:, lanes].astype(F32) * row_powers(rate, 0.0, 1.0, slab)
            local = dot_tn(decayed.astype(BF16), grad_out)
            for p in range(pieces):
                ret[h * pieces + p, :size] = local[p * size : (p + 1) * size]
        part = slice(first * pieces, (first + group) * pieces)
        lanes = lanes_of(first, group)
        stores.append(copies.start(ret.at[part, :size], ret_hbm.at[part, :size]))
        stores.append(copies.start(g.at[:, lanes], g_hbm.at[:, lanes]))
    gains = jnp.concatenate(gain_rows, axis=0)
    for j in range(heads * pieces):
        ret[j, size:] = gains
    stores.append(copies.start(ret.at[:, size:], ret_hbm.at[:, size:]))
    wait_all(stores)


def query_grad_kernel(
    per_step, slab, index_ref, k_ref, v_ref, g_ref, s_ref, o_ref, inv_ref, gain_ref, mixed_ref, qg_ref, inv_col
):
    step = pl.program_id(0)

    @pl.when(step == 0)
    def _():
        for b in range(slab // LANES):
            inv_col[lanes_of(b), :] = column(inv_ref[b : b + 1, :])

    for i in range(per_step):
        rate = rate_of(index_ref[step * per_step + i], slab)
        lanes = lanes_of(i)
        mixed_ref[0, :, lanes] = (o_ref[:, lanes] * inv_col[...] * gain_ref[:, lanes]).astype(BF16)
        k, v, g = head(k_ref, i), head(v_ref, i), g_ref[:, lanes]
        diagonal, below = decay_blocks(rate, False)
        carried = dot_nt(g, s_ref[i].astype(BF16)) * row_powers(rate, 1.0, 1.0, slab)
        a, b = slice(0, HALF), slice(HALF, 2 * HALF)
        upper = (dot_nt(g[a], v[a]) * diagonal).astype(BF16)
        lower = (dot_nt(g[b], v) * jnp.concatenate([below, diagonal], axis=1)).astype(BF16)
        qg_ref[0, a, lanes] = (dot_nn(upper, k[a]) + carried[a]).astype(BF16)
        qg_ref[0, b, lanes] = (dot_nn(lower, k) + carried[b]).astype(BF16)


def key_value_kernel(per_step, slab, index_ref, q_ref, k_ref, v_ref, g_ref, kl_ref, vl_ref):
    for i in range(per_step):
        rate = rate_of(index_ref[pl.program_id(0) * per_step + i], slab)
        lanes = lanes_of(i)
        q, k, v, g = head(q_ref, i), head(k_ref, i), head(v_ref, i), g_ref[:, lanes]
        diagonal, below = decay_blocks(rate, True)
        a, b = slice(0, HALF), slice(HALF, 2 * HALF)
        table = jnp.concatenate([diagonal, below], axis=1)
        for x, y, z, ref in ((v, g, q, kl_ref), (k, q, g, vl_ref)):
            first = (dot_nt(x[a], y) * table).astype(BF16)
            second = (dot_nt(x[b], y[b]) * diagonal).astype(BF16)
            ref[a, lanes] = dot_nn(first, z).astype(BF16)
            ref[b, lanes] = dot_nn(second, z[b]).astype(BF16)


def final_kernel(
    heads, group, slab, size, index_hbm, r_ref, k_hbm, v_hbm, kl, vl, own_ref, other_ref, kg_hbm, vg_hbm, gain_hbm,
    index, k, v, kg, vg, gain, semaphores,
):
    copies = Copies(semaphores)
    index_copy = copies.start(index_hbm, index)
    loads = []
    for first in range(0, heads, group):
        lanes = lanes_of(first, group)
        loads.append([copies.start(x.at[0, :, lanes], y.at[:, lanes]) for x, y in ((k_hbm, k), (v_hbm, v))])
    gain[...] = own_ref[...] + other_ref[...]
    pieces = LANES // size
    index_copy.wait()
    stores = [copies.start(gain, gain_hbm)]
    for first in range(0, heads, group):
        wait_all(loads[first // group])
        for h in range(first, first + group):
            lanes = lanes_of(h)
            to_next = row_powers(rate_of(index[h], slab), float(slab), -1.0, slab)
            back = jnp.concatenate([r_ref[h * pieces + p, :size] for p in range(pieces)], axis=0).astype(BF16)
            kg[:, lanes] = (kl[:, lanes].astype(F32) + dot_nt(v[:, lanes], back) * to_next).astype(BF16)
            vg[:, lanes] = (vl[:, lanes].astype(F32) + dot_nn(k[:, lanes], back) * to_next).astype(BF16)
        lanes = lanes_of(first, group)
        stores += [copies.start(x.at[:, lanes], y.at[0, :, lanes]) for x, y in ((kg, kg_hbm), (vg, vg_hbm))]
    wait_all(stores)


def on_device(query_rows, key_rows, value_rows, norm_gain, cotangent, loss_mask, importance, advantage, lengths, decay_index):
    _, slab, features = query_rows.shape
    heads = decay_index.shape[0]
    slabs = lax.axis_size("seq")
    place = lax.axis_index("seq").reshape(1)
    size = heads * LANES // slabs
    total_features = float(features * lax.axis_size("head"))
    per_step = 2
    steps = heads // per_step
    wide = per_step * LANES
    blocks = slab // LANES
    gain_row = from_hbm(norm_gain.reshape(1, features))
    decay_hbm, query, key, value, upstream = map(from_hbm, (decay_index, query_rows, key_rows, value_rows, cotangent))

    smem = pl.BlockSpec(memory_space=pltpu.SMEM)
    vmem = pl.BlockSpec(memory_space=pltpu.VMEM)
    anywhere = pl.BlockSpec(memory_space=pl.ANY)
    token = pl.BlockSpec((1, slab, wide), lambda i: (0, 0, i))
    flat = pl.BlockSpec((slab, wide), lambda i: (0, i))
    gain_spec = pl.BlockSpec((1, wide), lambda i: (0, i))
    state = pl.BlockSpec((per_step, LANES, LANES), lambda i: (i, 0, 0))
    token_row = pl.BlockSpec((blocks, LANES), lambda i: (0, 0))
    gain_out = pl.BlockSpec((heads, LANES), lambda i: (0, 0))
    token_f32 = pltpu.HBM((slab, features), F32)
    token_out = pltpu.HBM(query_rows.shape, BF16)
    state_out = pltpu.HBM((heads, LANES, LANES), F32)
    row_out = jax.ShapeDtypeStruct((blocks, LANES), F32)
    gain_f32 = jax.ShapeDtypeStruct((heads, LANES), F32)
    params = pltpu.CompilerParams(vmem_limit_bytes=24 * 1024 * 1024)

    def held(dtype):
        return pltpu.VMEM((slab, features), dtype)

    def semaphores(count):
        return pltpu.SemaphoreType.DMA((count,))

    index_held = pltpu.SMEM((heads,), jnp.int32)
    gain_held = pltpu.VMEM((1, features), F32)
    state_held = pltpu.VMEM((heads, LANES, LANES), F32)
    state_half = pltpu.VMEM((heads, LANES, LANES), BF16)
    columns = pltpu.VMEM((slab, LANES), F32)

    def over_slabs(pieces):
        return lax.all_to_all(pieces, "seq", 0, 0, tiled=True)

    group = 2
    state_local = pl.pallas_call(
        functools.partial(state_kernel, heads, slab),
        in_specs=[anywhere] * 3,
        out_specs=anywhere,
        out_shape=state_out,
        scratch_shapes=[index_held, held(BF16), held(BF16), state_held, semaphores(1 + 3 * heads)],
        compiler_params=params,
        name="state_local",
    )(decay_hbm, key, value)
    sent = over_slabs(state_local.reshape(slabs, size, LANES))

    local_out, weight = pl.pallas_call(
        functools.partial(local_kernel, per_step, slab, slab * slabs),
        grid=(steps,),
        in_specs=[smem, smem, smem, smem, token, token, token]
        + [pl.BlockSpec((1, slab), lambda i: (0, 0))] * 2,
        out_specs=[flat, token_row],
        out_shape=[pltpu.VMEM((slab, features), F32), row_out],
        compiler_params=params,
        name="local_attention",
    )(decay_index, place, lengths, advantage, query, key, value, loss_mask, importance)
    local_out = from_vmem(local_out)

    def scan(reverse, pieces, extra, name):
        shape = (slabs, size, LANES)
        return pl.pallas_call(
            functools.partial(scan_kernel, slabs, slab, size, reverse, 4),
            in_specs=[smem, smem, vmem],
            out_specs=[anywhere] + [vmem] * len(extra),
            out_shape=[pltpu.HBM(shape, F32), *extra],
            scratch_shapes=[pltpu.VMEM(shape, F32), semaphores(slabs // 4)],
            compiler_params=params,
            name=name,
        )(decay_index, place, pieces)

    (before,) = scan(False, sent, [], "prefix")
    state_in = over_slabs(before).reshape(heads, LANES, LANES)

    groups = lax.axis_size("head")
    outputs, query_held, grad_y, stats = pl.pallas_call(
        functools.partial(output_kernel, heads, slab),
        in_specs=[anywhere, anywhere, vmem, vmem, anywhere, vmem, anywhere],
        out_specs=[vmem] * 4,
        out_shape=[held(F32), held(BF16), held(F32), jax.ShapeDtypeStruct((groups, 2 * blocks, LANES), F32)],
        scratch_shapes=[index_held, gain_held, held(BF16), state_half, semaphores(2 + 2 * blocks)],
        compiler_params=params,
        name="outputs",
    )(decay_hbm, query, state_in, local_out, upstream, weight, gain_row)
    stats = lax.all_to_all(stats, "head", 0, 0, tiled=True)

    return_shape = (slabs, size + heads, LANES)
    grad_out, outputs, return_local, inverse = pl.pallas_call(
        functools.partial(grad_kernel, heads, group, slab, total_features, size),
        in_specs=[anywhere, vmem, vmem, vmem, vmem, anywhere],
        out_specs=[anywhere, anywhere, anywhere, vmem],
        out_shape=[pltpu.HBM((slab, features), BF16), token_f32, pltpu.HBM(return_shape, F32), row_out],
        scratch_shapes=[
            index_held, gain_held, held(BF16), pltpu.VMEM(return_shape, F32), columns, columns,
            semaphores(4 + 2 * heads // group),
        ],
        compiler_params=params,
        name="output_grad",
    )(decay_hbm, stats, from_vmem(query_held), from_vmem(outputs), from_vmem(grad_y), gain_row)
    grad_out, outputs = from_hbm(grad_out), from_hbm(outputs)
    returned = over_slabs(return_local)

    mixed, query_grad = pl.pallas_call(
        functools.partial(query_grad_kernel, per_step, slab),
        grid=(steps,),
        in_specs=[smem, token, token, flat, state, flat, token_row, gain_spec],
        out_specs=[token, token],
        out_shape=[token_out, token_out],
        scratch_shapes=[columns],
        compiler_params=params,
        name="query_grads",
    )(decay_index, key, value, grad_out, state_in, outputs, inverse, gain_row)
    returned, mixed, query_grad = lax.optimization_barrier((returned, mixed, query_grad))
    after, gain_sum = scan(True, returned, [gain_f32], "suffix")
    return_in = over_slabs(after)

    key_local, value_local = pl.pallas_call(
        functools.partial(key_value_kernel, per_step, slab),
        grid=(steps,),
        in_specs=[smem, token, token, token, flat],
        out_specs=[flat, flat],
        out_shape=[held(BF16), held(BF16)],
        compiler_params=params,
        name="key_value_grads",
    )(decay_index, query, key, value, grad_out)

    gain_sum, key_local, value_local = lax.optimization_barrier((gain_sum, key_local, value_local))
    other_sum = lax.ppermute(gain_sum, "dp", [(i, 1 - i) for i in range(2)])
    key_grad, value_grad, gain_grad = pl.pallas_call(
        functools.partial(final_kernel, heads, group, slab, size),
        in_specs=[anywhere, vmem, anywhere, anywhere, vmem, vmem, vmem, vmem],
        out_specs=[anywhere] * 3,
        out_shape=[token_out, token_out, pltpu.HBM((heads, LANES), F32)],
        scratch_shapes=[index_held] + [held(BF16)] * 4
        + [pltpu.VMEM((heads, LANES), F32), semaphores(2 + 4 * heads // group)],
        compiler_params=params,
        name="final_grads",
    )(decay_hbm, return_in, key, value, from_vmem(key_local), from_vmem(value_local), gain_sum, other_sum)
    return (mixed, query_grad, key_grad, value_grad, gain_grad.reshape(features))


def solution(mesh):
    tokens = P("dp", "seq", "head")
    return jax.shard_map(
        on_device,
        mesh=mesh,
        in_specs=(
            tokens, tokens, tokens, P("head"), tokens, P("dp", "seq"), P("dp", "seq"), P("dp"), P("dp"), P("head"),
        ),
        out_specs=(tokens, tokens, tokens, tokens, P("head")),
        check_vma=False,
    )
```

```python
import functools

import jax
import jax.numpy as jnp
from jax import lax
from jax.experimental import pallas as pl
from jax.experimental.pallas import tpu as pltpu
from jax.sharding import PartitionSpec as P

clip_high = 1.28
epsilon = 1e-06
F32 = jnp.float32
BF16 = jnp.bfloat16
LANES = 128
HALF = 256


def dot_nn(a, b):
    return lax.dot_general(a, b, (((1,), (0,)), ((), ())), preferred_element_type=F32)


def dot_nt(a, b):
    return lax.dot_general(a, b, (((1,), (1,)), ((), ())), preferred_element_type=F32)


def dot_tn(a, b):
    return lax.dot_general(a, b, (((0,), (0,)), ((), ())), preferred_element_type=F32)


def rate_of(index, slab):
    return (16.0 / slab) * jnp.exp2(jnp.full((1, LANES), -index.astype(F32), F32))


def row_powers(rate, first, step, rows):
    at = lax.broadcasted_iota(jnp.int32, (LANES, LANES), 0).astype(F32)
    powers = jnp.exp2(-rate * (first + step * at))
    parts = [powers] + [powers * jnp.exp2(-rate * (step * b)) for b in range(LANES, rows, LANES)]
    return jnp.concatenate(parts, axis=0) if len(parts) > 1 else powers


def decay_blocks(rate, transposed):
    rate2 = jnp.concatenate([rate] * (HALF // LANES), axis=1)
    rows = lax.broadcasted_iota(jnp.int32, (HALF, HALF), 0)
    cols = lax.broadcasted_iota(jnp.int32, (HALF, HALF), 1)
    lag = (cols - rows if transposed else rows - cols).astype(F32)
    powers = jnp.exp2(-rate2 * lag)
    return jnp.where(lag >= 0, powers, 0.0), powers * jnp.exp2(-rate2 * float(HALF))


def head(ref, i):
    return ref[0, :, i * LANES : (i + 1) * LANES]


def from_vmem(x):
    return pltpu.with_memory_space_constraint(x, pltpu.VMEM)


def from_hbm(x):
    return pltpu.with_memory_space_constraint(x, pltpu.HBM)


class Copies:
    def __init__(self, semaphores):
        self.semaphores = semaphores
        self.used = 0

    def start(self, source, target):
        copy = pltpu.make_async_copy(source, target, self.semaphores.at[self.used])
        self.used += 1
        copy.start()
        return copy


def wait_all(copies):
    for copy in copies:
        copy.wait()


def lanes_of(first, count=1):
    return slice(first * LANES, (first + count) * LANES)


def column(row):
    return jnp.broadcast_to(row, (LANES, LANES)).T


def state_kernel(heads, slab, index_hbm, k_hbm, v_hbm, out_hbm, rates, index, k, v, out, semaphores):
    copies = Copies(semaphores)
    index_copy = copies.start(index_hbm, index)
    spans = [slice(at, at + HALF) for at in range(0, slab, HALF)]
    loads = [[copies.start(x.at[0, rows], y.at[rows]) for x, y in ((k_hbm, k), (v_hbm, v))] for rows in spans]
    stores = []
    index_copy.wait()
    for h in range(heads):
        rates[h : h + 1, :] = rate_of(index[h], slab)
    for rows, load in zip(spans, loads):
        wait_all(load)
        for h in range(heads):
            powers = row_powers(rates[h : h + 1, :], slab - 1.0 - rows.start, -1.0, HALF)
            decayed = (k[rows, lanes_of(h)].astype(F32) * powers).astype(BF16)
            term = dot_tn(decayed, v[rows, lanes_of(h)])
            out[h] = term if rows.start == 0 else out[h] + term
            if rows.stop == slab and h % 4 == 3:
                part = slice(h - 3, h + 1)
                stores.append(copies.start(out.at[part], out_hbm.at[part]))
    wait_all(stores)


def scan_kernel(slabs, slab, size, reverse, group, place_ref, rates_ref, x_ref, out_hbm, *refs):
    extra, (out, semaphores) = refs[:-2], refs[-2:]
    copies = Copies(semaphores)
    rate = rates_ref[pl.ds((place_ref[0] * size) // LANES, 1), :]
    factor = jnp.exp2(-rate * float(slab))
    running = jnp.zeros((size, LANES), F32)
    order = list(reversed(range(slabs))) if reverse else list(range(slabs))
    stores = []
    for at in range(0, slabs, group):
        for j in order[at : at + group]:
            out[j] = running
            running = factor * running + x_ref[j, :size]
        part = slice(min(order[at : at + group]), max(order[at : at + group]) + 1)
        stores.append(copies.start(out.at[part], out_hbm.at[part]))
    if extra:
        total = x_ref[0, size:]
        for j in range(1, slabs):
            total += x_ref[j, size:]
        extra[0][...] = total
    wait_all(stores)


def local_kernel(
    per_step, slab, total, place_ref, length_ref, advantage_ref, rates_ref, q_ref, k_ref, v_ref, c_ref, mask_ref, imp_ref,
    out_ref, weight_ref, q_first_ref, c_first_ref,
):
    @pl.when(pl.program_id(0) == 0)
    def _():
        at = place_ref[0] * slab + lax.broadcasted_iota(jnp.int32, (1, slab), 1)
        length = length_ref[...]
        inside = (at < length).astype(F32)
        weight = mask_ref[...].astype(F32) * inside * jnp.minimum(imp_ref[...], clip_high)
        weight = weight * advantage_ref[...] * (float(total) / length.astype(F32))
        for b in range(slab // LANES):
            weight_ref[b : b + 1, :] = weight[:, lanes_of(b)]

    q_first_ref[...] = q_ref[0, :LANES, :]
    c_first_ref[...] = c_ref[0]
    for i in range(per_step):
        rate = rates_ref[pl.ds(pl.program_id(0) * per_step + i, 1), :]
        diagonal, below = decay_blocks(rate, False)
        q, k, v = head(q_ref, i), head(k_ref, i), head(v_ref, i)
        lanes = lanes_of(i)
        for r in range(slab // HALF):
            scores = dot_nt(q[r * HALF : (r + 1) * HALF], k[: (r + 1) * HALF])
            table = diagonal if r == 0 else jnp.concatenate([below, diagonal], axis=1)
            probs = (scores * table).astype(BF16)
            out_ref[r * HALF : (r + 1) * HALF, lanes] = dot_nn(probs, v[: (r + 1) * HALF])


def output_kernel(
    heads, slab, rates, q_hbm, s_ref, local, c_hbm, weight_ref, gain, q_first, c_first, out, q, grad_y, stat_ref,
    c, s, semaphores,
):
    copies = Copies(semaphores)
    spans = [(0, 1), (1, 1), (2, slab // LANES - 2)]
    loads = [[]]
    for first, count in spans[1:]:
        rows = lanes_of(first, count)
        loads.append([copies.start(q_hbm.at[0, rows], q.at[rows]), copies.start(c_hbm.at[0, rows], c.at[rows])])
    q[:LANES] = q_first[...]
    c[:LANES] = c_first[...]
    for h in range(heads):
        s[h] = s_ref[h].astype(BF16)
    square_rows, cross_rows = [], []
    for (first, count), load in zip(spans, loads):
        rows = lanes_of(first, count)
        weight = jnp.concatenate([column(weight_ref[x : x + 1, :]) for x in range(first, first + count)], axis=0)
        squares = jnp.zeros((count * LANES, LANES), F32)
        crosses = jnp.zeros((count * LANES, LANES), F32)
        wait_all(load)
        for h in range(heads):
            lanes = lanes_of(h)
            carried = dot_nn(q[rows, lanes], s[h])
            o = local[rows, lanes] + carried * row_powers(rates[h : h + 1, :], first * LANES + 1.0, 1.0, count * LANES)
            out[rows, lanes] = o
            squares += o * o
            grad = c[rows, lanes].astype(F32) * weight
            grad_y[rows, lanes] = grad
            crosses += (grad * gain[:, lanes]) * o
        for x in range(count):
            square_rows.append(jnp.sum(squares[lanes_of(x)].T, axis=0, keepdims=True))
            cross_rows.append(jnp.sum(crosses[lanes_of(x)].T, axis=0, keepdims=True))
    stats = jnp.concatenate(square_rows + cross_rows, axis=0)
    for d in range(stat_ref.shape[0]):
        stat_ref[d] = stats


def grad_kernel(
    heads, group, slab, features, size, rates, stat_ref, q, o, grad_y, gain,
    g_hbm, o_hbm, ret_hbm, inv_ref, g, ret, inv_col, mean_col, semaphores,
):
    copies = Copies(semaphores)
    stores = [copies.start(o, o_hbm)]
    stats = jnp.sum(stat_ref[...], axis=0)
    blocks = slab // LANES
    inverse = lax.rsqrt(stats[:blocks] / features + epsilon)
    mean = stats[blocks : 2 * blocks] * inverse / features
    inv_ref[...] = inverse
    for b in range(blocks):
        rows = lanes_of(b)
        inv_col[rows, :] = column(inverse[b : b + 1])
        mean_col[rows, :] = column(mean[b : b + 1])
    pieces = LANES // size
    gain_rows = []
    for first in range(0, heads, group):
        for h in range(first, first + group):
            rate = rates[h : h + 1, :]
            lanes = lanes_of(h)
            normed = o[:, lanes] * inv_col[...]
            gain_rows.append(jnp.sum(grad_y[:, lanes] * normed, axis=0, keepdims=True))
            grad_n = grad_y[:, lanes] * gain[:, lanes]
            grad_out = (inv_col[...] * (grad_n - normed * mean_col[...])).astype(BF16)
            g[:, lanes] = grad_out
            decayed = q[:, lanes].astype(F32) * row_powers(rate, 0.0, 1.0, slab)
            local = dot_tn(decayed.astype(BF16), grad_out)
            for p in range(pieces):
                ret[h * pieces + p, :size] = local[p * size : (p + 1) * size]
        part = slice(first * pieces, (first + group) * pieces)
        lanes = lanes_of(first, group)
        stores.append(copies.start(ret.at[part, :size], ret_hbm.at[part, :size]))
        stores.append(copies.start(g.at[:, lanes], g_hbm.at[:, lanes]))
    gains = jnp.concatenate(gain_rows, axis=0)
    for j in range(heads * pieces):
        ret[j, size:] = gains
    stores.append(copies.start(ret.at[:, size:], ret_hbm.at[:, size:]))
    wait_all(stores)


def query_grad_kernel(
    per_step, slab, rates_ref, k_ref, v_ref, g_ref, s_ref, o_ref, inv_ref, gain_ref, mixed_ref, qg_ref, inv_col
):
    step = pl.program_id(0)

    @pl.when(step == 0)
    def _():
        for b in range(slab // LANES):
            inv_col[lanes_of(b), :] = column(inv_ref[b : b + 1, :])

    for i in range(per_step):
        rate = rates_ref[pl.ds(step * per_step + i, 1), :]
        lanes = lanes_of(i)
        mixed_ref[0, :, lanes] = (o_ref[:, lanes] * inv_col[...] * gain_ref[:, lanes]).astype(BF16)
        k, v, g = head(k_ref, i), head(v_ref, i), g_ref[:, lanes]
        diagonal, below = decay_blocks(rate, False)
        carried = dot_nt(g, s_ref[i].astype(BF16)) * row_powers(rate, 1.0, 1.0, slab)
        a, b = slice(0, HALF), slice(HALF, 2 * HALF)
        upper = (dot_nt(g[a], v[a]) * diagonal).astype(BF16)
        lower = (dot_nt(g[b], v) * jnp.concatenate([below, diagonal], axis=1)).astype(BF16)
        qg_ref[0, a, lanes] = (dot_nn(upper, k[a]) + carried[a]).astype(BF16)
        qg_ref[0, b, lanes] = (dot_nn(lower, k) + carried[b]).astype(BF16)


def key_value_kernel(
    per_step, slab, rates_ref, q_ref, k_ref, v_ref, g_ref, kl_ref, vl_ref, k_first_ref, v_first_ref
):
    @pl.when(pl.program_id(0) == 0)
    def _():
        k_first_ref[...] = k_ref[0]
        v_first_ref[...] = v_ref[0]

    for i in range(per_step):
        rate = rates_ref[pl.ds(pl.program_id(0) * per_step + i, 1), :]
        lanes = lanes_of(i)
        q, k, v, g = head(q_ref, i), head(k_ref, i), head(v_ref, i), g_ref[:, lanes]
        diagonal, below = decay_blocks(rate, True)
        a, b = slice(0, HALF), slice(HALF, 2 * HALF)
        table = jnp.concatenate([diagonal, below], axis=1)
        for x, y, z, ref in ((v, g, q, kl_ref), (k, q, g, vl_ref)):
            first = (dot_nt(x[a], y) * table).astype(BF16)
            second = (dot_nt(x[b], y[b]) * diagonal).astype(BF16)
            ref[a, lanes] = dot_nn(first, z).astype(BF16)
            ref[b, lanes] = dot_nn(second, z[b]).astype(BF16)


def final_kernel(
    heads, group, slab, size, rates, r_ref, k_hbm, v_hbm, kl, vl, k_first, v_first, own_ref, other_ref,
    kg_hbm, vg_hbm, gain_hbm, k, v, kg, vg, gain, semaphores,
):
    copies = Copies(semaphores)
    loads = [[]]
    for first in range(group, heads, group):
        lanes = lanes_of(first, group)
        loads.append([copies.start(x.at[0, :, lanes], y.at[:, lanes]) for x, y in ((k_hbm, k), (v_hbm, v))])
    gain[...] = own_ref[...] + other_ref[...]
    pieces = LANES // size
    stores = [copies.start(gain, gain_hbm)]
    for first in range(0, heads, group):
        wait_all(loads[first // group])
        source = (k_first, v_first) if first == 0 else (k, v)
        for h in range(first, first + group):
            lanes = lanes_of(h)
            to_next = row_powers(rates[h : h + 1, :], float(slab), -1.0, slab)
            back = jnp.concatenate([r_ref[h * pieces + p, :size] for p in range(pieces)], axis=0).astype(BF16)
            kg[:, lanes] = (kl[:, lanes].astype(F32) + dot_nt(source[1][:, lanes], back) * to_next).astype(BF16)
            vg[:, lanes] = (vl[:, lanes].astype(F32) + dot_nn(source[0][:, lanes], back) * to_next).astype(BF16)
        lanes = lanes_of(first, group)
        stores += [copies.start(x.at[:, lanes], y.at[0, :, lanes]) for x, y in ((kg, kg_hbm), (vg, vg_hbm))]
    wait_all(stores)


def on_device(query_rows, key_rows, value_rows, norm_gain, cotangent, loss_mask, importance, advantage, lengths, decay_index):
    _, slab, features = query_rows.shape
    heads = decay_index.shape[0]
    slabs = lax.axis_size("seq")
    place = lax.axis_index("seq").reshape(1)
    size = heads * LANES // slabs
    total_features = float(features * lax.axis_size("head"))
    per_step = 2
    steps = heads // per_step
    wide = per_step * LANES
    blocks = slab // LANES
    gain_row = norm_gain.reshape(1, features)
    decay_hbm, query, key, value, upstream = map(from_hbm, (decay_index, query_rows, key_rows, value_rows, cotangent))

    smem = pl.BlockSpec(memory_space=pltpu.SMEM)
    vmem = pl.BlockSpec(memory_space=pltpu.VMEM)
    anywhere = pl.BlockSpec(memory_space=pl.ANY)
    token = pl.BlockSpec((1, slab, wide), lambda i: (0, 0, i))
    flat = pl.BlockSpec((slab, wide), lambda i: (0, i))
    gain_spec = pl.BlockSpec((1, wide), lambda i: (0, i))
    state = pl.BlockSpec((per_step, LANES, LANES), lambda i: (i, 0, 0))
    token_row = pl.BlockSpec((blocks, LANES), lambda i: (0, 0))
    gain_out = pl.BlockSpec((heads, LANES), lambda i: (0, 0))
    one = pl.BlockSpec((1, slab), lambda i: (0, 0))
    token_f32 = pltpu.HBM((slab, features), F32)
    token_out = pltpu.HBM(query_rows.shape, BF16)
    state_out = pltpu.HBM((heads, LANES, LANES), F32)
    row_out = jax.ShapeDtypeStruct((blocks, LANES), F32)
    gain_f32 = jax.ShapeDtypeStruct((heads, LANES), F32)
    params = pltpu.CompilerParams(vmem_limit_bytes=24 * 1024 * 1024)

    def held(dtype):
        return pltpu.VMEM((slab, features), dtype)

    def semaphores(count):
        return pltpu.SemaphoreType.DMA((count,))

    index_held = pltpu.SMEM((heads,), jnp.int32)
    state_held = pltpu.VMEM((heads, LANES, LANES), F32)
    state_half = pltpu.VMEM((heads, LANES, LANES), BF16)
    columns = pltpu.VMEM((slab, LANES), F32)

    def over_slabs(pieces):
        return lax.all_to_all(pieces, "seq", 0, 0, tiled=True)

    group = 2
    state_local, rates = pl.pallas_call(
        functools.partial(state_kernel, heads, slab),
        in_specs=[anywhere] * 3,
        out_specs=[anywhere, vmem],
        out_shape=[state_out, gain_f32],
        scratch_shapes=[index_held, held(BF16), held(BF16), state_held, semaphores(1 + 3 * heads)],
        compiler_params=params,
        name="state_local",
    )(decay_hbm, key, value)
    sent = over_slabs(state_local.reshape(slabs, size, LANES))
    length_row = jnp.broadcast_to(lengths.reshape(1, 1), (1, slab))
    advantage_row = jnp.broadcast_to(advantage.reshape(1, 1), (1, slab))
    sent, length_row, advantage_row = lax.optimization_barrier((sent, length_row, advantage_row))

    first_rows = pltpu.VMEM((LANES, features), BF16)
    local_out, weight, query_first, upstream_first = pl.pallas_call(
        functools.partial(local_kernel, per_step, slab, slab * slabs),
        grid=(steps,),
        in_specs=[smem, one, one, gain_out, token, token, token, pl.BlockSpec((1, LANES, wide), lambda i: (0, 0, i))]
        + [pl.BlockSpec((1, slab), lambda i: (0, 0))] * 2,
        out_specs=[flat, token_row] + [pl.BlockSpec((LANES, wide), lambda i: (0, i))] * 2,
        out_shape=[held(F32), row_out, first_rows, first_rows],
        compiler_params=params,
        name="local_attention",
    )(
        place, length_row, advantage_row, rates, query, key, value, upstream, loss_mask, importance
    )
    local_out = from_vmem(local_out)

    def scan(reverse, pieces, extra, name):
        shape = (slabs, size, LANES)
        return pl.pallas_call(
            functools.partial(scan_kernel, slabs, slab, size, reverse, 4),
            in_specs=[smem, vmem, vmem],
            out_specs=[anywhere] + [vmem] * len(extra),
            out_shape=[pltpu.HBM(shape, F32), *extra],
            scratch_shapes=[pltpu.VMEM(shape, F32), semaphores(slabs // 4)],
            compiler_params=params,
            name=name,
        )(place, rates, pieces)

    (before,) = scan(False, sent, [], "prefix")
    state_in = over_slabs(before).reshape(heads, LANES, LANES)

    groups = lax.axis_size("head")
    outputs, query_held, grad_y, stats = pl.pallas_call(
        functools.partial(output_kernel, heads, slab),
        in_specs=[vmem, anywhere, vmem, vmem, anywhere, vmem, vmem, vmem, vmem],
        out_specs=[vmem] * 4,
        out_shape=[held(F32), held(BF16), held(F32), jax.ShapeDtypeStruct((groups, 2 * blocks, LANES), F32)],
        scratch_shapes=[held(BF16), state_half, semaphores(4)],
        compiler_params=params,
        name="outputs",
    )(
        rates, query, state_in, local_out, upstream, weight, gain_row, from_vmem(query_first), from_vmem(upstream_first)
    )
    stats = lax.all_to_all(stats, "head", 0, 0, tiled=True)

    return_shape = (slabs, size + heads, LANES)
    grad_out, outputs, return_local, inverse = pl.pallas_call(
        functools.partial(grad_kernel, heads, group, slab, total_features, size),
        in_specs=[vmem] * 6,
        out_specs=[anywhere, anywhere, anywhere, vmem],
        out_shape=[pltpu.HBM((slab, features), BF16), token_f32, pltpu.HBM(return_shape, F32), row_out],
        scratch_shapes=[
            held(BF16), pltpu.VMEM(return_shape, F32), columns, columns, semaphores(2 + 2 * heads // group)
        ],
        compiler_params=params,
        name="output_grad",
    )(rates, stats, from_vmem(query_held), from_vmem(outputs), from_vmem(grad_y), gain_row)
    grad_out, outputs = from_hbm(grad_out), from_hbm(outputs)
    returned = over_slabs(return_local)

    mixed, query_grad = pl.pallas_call(
        functools.partial(query_grad_kernel, per_step, slab),
        grid=(steps,),
        in_specs=[gain_out, token, token, flat, state, flat, token_row, gain_spec],
        out_specs=[token, token],
        out_shape=[token_out, token_out],
        scratch_shapes=[columns],
        compiler_params=params,
        name="query_grads",
    )(rates, key, value, grad_out, state_in, outputs, inverse, gain_row)
    returned, mixed, query_grad = lax.optimization_barrier((returned, mixed, query_grad))
    after, gain_sum = scan(True, returned, [gain_f32], "suffix")
    return_in = over_slabs(after)

    first_heads = pltpu.VMEM((slab, wide), BF16)
    key_local, value_local, key_first, value_first = pl.pallas_call(
        functools.partial(key_value_kernel, per_step, slab),
        grid=(steps,),
        in_specs=[gain_out, token, token, token, flat],
        out_specs=[flat, flat] + [pl.BlockSpec((slab, wide), lambda i: (0, 0))] * 2,
        out_shape=[held(BF16), held(BF16), first_heads, first_heads],
        compiler_params=params,
        name="key_value_grads",
    )(rates, query, key, value, grad_out)

    gain_sum, key_local, value_local = lax.optimization_barrier((gain_sum, key_local, value_local))
    other_sum = lax.ppermute(gain_sum, "dp", [(i, 1 - i) for i in range(2)])
    key_grad, value_grad, gain_grad = pl.pallas_call(
        functools.partial(final_kernel, heads, per_step, slab, size),
        in_specs=[vmem, vmem, anywhere, anywhere] + [vmem] * 6,
        out_specs=[anywhere] * 3,
        out_shape=[token_out, token_out, pltpu.HBM((heads, LANES), F32)],
        scratch_shapes=[held(BF16)] * 4 + [pltpu.VMEM((heads, LANES), F32), semaphores(1 + 4 * steps)],
        compiler_params=params,
        name="final_grads",
    )(
        rates, return_in, key, value, from_vmem(key_local), from_vmem(value_local), from_vmem(key_first),
        from_vmem(value_first), gain_sum, other_sum,
    )
    return (mixed, query_grad, key_grad, value_grad, gain_grad.reshape(features))


def solution(mesh):
    tokens = P("dp", "seq", "head")
    return jax.shard_map(
        on_device,
        mesh=mesh,
        in_specs=(
            tokens, tokens, tokens, P("head"), tokens, P("dp", "seq"), P("dp", "seq"), P("dp"), P("dp"), P("head"),
        ),
        out_specs=(tokens, tokens, tokens, tokens, P("head")),
        check_vma=False,
    )
```
